1024 devices in a mesh: blk: 32 (over y, z_lo), ulysses: 32 (over z_hi, x, core).
Axes of the slice: x: 8, y: 8, z: 8 (z_hi: 2, z_lo: 4; z = z_hi * 4 + z_lo), core: 2. Of those that a mesh axis runs over, the one named last changes fastest.
Arguments:
- queries: bfloat16 [6144, 4096], P(('blk', 'ulysses')), may hold values from -8 to 8
- key_vectors: bfloat16 [6144, 4096], P(('blk', 'ulysses')), may hold values from -8 to 8
- value_vectors: bfloat16 [6144, 4096], P(('blk', 'ulysses')), may hold values from -12 to 12
- cotangent: bfloat16 [6144, 4096], P(('blk', 'ulysses')), may hold values from -192 to 192
Outputs:
- grad_queries: bfloat16 [6144, 4096], P(('blk', 'ulysses'))
- grad_keys: bfloat16 [6144, 4096], P(('blk', 'ulysses'))
- grad_values: bfloat16 [6144, 4096], P(('blk', 'ulysses'))
The draws below stay inside these ranges and needn't reach their ends.
All inputs are finite; a program needn't handle non-finite values.
Results may differ from the reference program's by a relative error of at most 0.0067.
Values may be sent and summed in bfloat16 or wider, within the bound.
A program may use at most 64 MiB of HBM per device.

```python
import math
import jax
import jax.numpy as jnp
from jax import lax

HEADS = 32
D_HEAD = 128
TOKENS = 6144


def drawn_draw(key, which_arg):
    columns = HEADS * D_HEAD
    noise_key = jax.random.fold_in(key, 101 + which_arg)
    result_array = jnp.clip(jax.random.normal(noise_key, (TOKENS, columns), jnp.float32), -5.0, 5.0)
    return result_array.astype(jnp.bfloat16)


def draw_queries(key, part):
    return drawn_draw(key, 0)


def draw_key_vectors(key, part):
    return drawn_draw(key, 1)


def shard_levels(rng, dims, cuts, smallest, high):
    def one(dim, parts):
        draws = jax.random.uniform(jax.random.fold_in(jax.random.fold_in(rng, 6), dim), (parts,), jnp.float32, smallest / len(cuts), high / len(cuts))
        return jnp.repeat(jnp.exp(draws), dims[dim] // parts).reshape((-1,) + (1,) * (len(dims) - dim - 1))

    gain = one(*cuts[0])
    for cut in cuts[1:]:
        gain = gain * one(*cut)
    return gain


def scatter_about(own_key, dims, deviation, most, split=(), held_as=jnp.bfloat16):
    array = jax.random.normal(own_key, dims, jnp.float32) * deviation
    if len(split) > 0:
        array = shard_levels(own_key, dims, split, -0.22, 0.18) * array
    return jnp.clip(array, min=-most, max=most).astype(held_as)


def setup_inputs(seed: int = 0) -> dict:
    streams_of = jax.random.split(jax.random.key(seed), 5)
    return {
        "queries": draw_queries(jax.random.fold_in(streams_of[4], 71), 0),
        "key_vectors": draw_key_vectors(jax.random.fold_in(streams_of[4], 71), 0),
        "value_vectors": scatter_about(streams_of[2], (TOKENS, HEADS * D_HEAD), 2.0, 12.0, ((0, 1024),)),
        "cotangent": scatter_about(streams_of[3], (TOKENS, HEADS * D_HEAD), 32.0, 192.0, ((0, 1024),)),
    }


def one_head(operands):
    query_head, key_head, value_head, grad_head = operands
    score_scale = 1.0 / math.sqrt(D_HEAD)
    logits = jnp.dot(query_head, key_head.T, preferred_element_type=jnp.float32) * score_scale
    row_top = lax.optimization_barrier(jnp.max(logits, axis=1, keepdims=True))
    log_total = row_top + jnp.log(lax.optimization_barrier(jnp.sum(jnp.exp(logits - row_top), axis=1, keepdims=True)))
    weights = jnp.exp(logits - log_total)
    grad_weights = jnp.dot(grad_head, value_head.T, preferred_element_type=jnp.float32)
    row_dot = lax.optimization_barrier(jnp.sum(weights * grad_weights, axis=1, keepdims=True))
    grad_logits = weights * (grad_weights - row_dot)
    weights_low = weights.astype(jnp.bfloat16)
    grad_low = grad_logits.astype(jnp.bfloat16)
    grad_query = (jnp.dot(grad_low, key_head, preferred_element_type=jnp.float32) * score_scale).astype(jnp.bfloat16)
    grad_key = (jnp.dot(grad_low.T, query_head, preferred_element_type=jnp.float32) * score_scale).astype(jnp.bfloat16)
    grad_value = jnp.dot(weights_low.T, grad_head, preferred_element_type=jnp.float32).astype(jnp.bfloat16)
    return (grad_query, grad_key, grad_value)

def reference(queries, key_vectors, value_vectors, cotangent):

    def heads_first(matrix):
        return matrix.reshape(TOKENS, HEADS, D_HEAD).transpose(1, 0, 2)

    def rows_first(stacked):
        return stacked.transpose(1, 0, 2).reshape(TOKENS, HEADS * D_HEAD)
    grads = lax.map(one_head, (heads_first(queries), heads_first(key_vectors), heads_first(value_vectors), heads_first(cotangent)))
    return (rows_first(grads[0]), rows_first(grads[1]), rows_first(grads[2]))
```

```python
import functools
import math

import jax
import jax.numpy as jnp
import numpy as np
from jax import lax
from jax.experimental import pallas as pl
from jax.experimental.pallas import tpu as pltpu
from jax.sharding import PartitionSpec as P

D = 128
NQ = 8
NK = 4
NP = NQ // 2
F32 = jnp.float32
BF16 = jnp.bfloat16
GROUP = 8


def dot_nt(a, b):
    return lax.dot_general(a, b, (((1,), (1,)), ((), ())), preferred_element_type=F32)


def log2(x):
    return jnp.log(x) * (1.0 / math.log(2.0))


def q_mask(k):
    return (k >> 1) & 1, (k & 1) | ((k >> 2) & 1) << 1


def k_mask(j):
    return (j & 1) << 2 | (j >> 1) << 1, 0


def h_mask(i):
    iz, ix, iy = i >> 4, (i >> 2) & 3, i & 3
    mb = iy << 3 | (4 if iy == 2 else 0) | (3 if iz else 0)
    mu = iz << 4 | ix << 2 | (2 if ix == 2 else 0)
    return mb, mu


def kernel(
    nu, t, q_hbm, k_hbm, v_hbm, g_hbm, sort_hbm, unsort_hbm, dq_ref, dk_ref, dv_ref,
    stage, sort_ref, unsort_ref, sbuf, rbuf, qg, kv, e_s, gw_s, gl_s, mlr, fin, st_send, st_all,
    dq_send, dq_recv, dkv_send, dkv_recv, osend, orecv,
    stage_sem, sort_sem, a2a_send, a2a_recv, kv_ssem, kv_rsem, qg_ssem, qg_rsem,
    st_ssem, st_rsem, dq_ssem, dq_rsem, dkv_ssem, dkv_rsem, out_send, out_recv,
):
    rows = nu * t
    cols = 2 * rows
    pack = 4 * t
    u = lax.axis_index("ulysses")
    blk = lax.axis_index("blk")
    scale = 1.0 / math.sqrt(D)
    scale2 = scale * math.log2(math.e)

    def flips(value):
        return [(1 - 2 * ((value // (1 << b)) % 2)) * (1 << b) for b in range(5)]

    def flipped(value, flip, mask):
        for b in range(5):
            if mask >> b & 1:
                value = value + flip[b]
        return value

    blk_flip, u_flip = flips(blk), flips(u)
    head = (u // 16) * 16 + ((u // 4) % 4) * 4 + blk // 8
    head_flip = flips(head)

    def peer(masks):
        return {"blk": flipped(blk, blk_flip, masks[0]), "ulysses": flipped(u, u_flip, masks[1])}

    def remote(src, dst, ssem, rsem, masks):
        return pltpu.make_async_remote_copy(
            src_ref=src, dst_ref=dst, send_sem=ssem, recv_sem=rsem,
            device_id=peer(masks), device_id_type=pl.DeviceIdType.MESH,
        )

    loads = [
        pltpu.make_async_copy(src, stage.at[a], stage_sem.at[a])
        for a, src in enumerate((q_hbm, k_hbm, v_hbm, g_hbm))
    ]
    loads.append(pltpu.make_async_copy(sort_hbm, sort_ref, sort_sem.at[0]))
    loads.append(pltpu.make_async_copy(unsort_hbm, unsort_ref, sort_sem.at[1]))
    for c in loads:
        c.start()

    barrier = pltpu.get_barrier_semaphore()
    partners = [h_mask(i) for i in range(1, nu)]
    partners += [q_mask(k) for k in range(1, NQ)] + [k_mask(j) for j in range(1, NK)]
    for masks in partners:
        pl.semaphore_signal(
            barrier, inc=1, device_id=peer(masks), device_id_type=pl.DeviceIdType.MESH
        )

    for c in loads:
        c.wait()
    packed = jnp.concatenate([stage[a].astype(F32) for a in range(4)], axis=0).astype(BF16)
    for h in range(nu):
        sbuf[h] = packed[:, h * D : (h + 1) * D]
    rbuf[0] = sbuf[head]

    pl.semaphore_wait(barrier, len(partners))

    for i in range(nu - 1, 0, -1):
        remote(
            sbuf.at[flipped(head, head_flip, i)], rbuf.at[i], a2a_send, a2a_recv, h_mask(i)
        ).start()
    pltpu.make_async_copy(
        rbuf.at[pl.ds(0, nu - 1)], rbuf.at[pl.ds(0, nu - 1)], a2a_recv
    ).wait()

    piece = GROUP * t
    for m in range(nu // GROUP):
        x = rbuf[m * GROUP : (m + 1) * GROUP].reshape(GROUP * pack, D)
        s = jnp.dot(sort_ref[...], x, preferred_element_type=F32).astype(BF16)
        lo, hi = m * piece, (m + 1) * piece
        qg[0, 0, lo:hi, :] = s[0:piece]
        kv[0, 0, lo:hi, :] = s[piece : 2 * piece]
        kv[1, 0, lo:hi, :] = s[2 * piece : 3 * piece]
        qg[1, 0, lo:hi, :] = s[3 * piece : 4 * piece]

    def q_slot(a, k):
        return qg.at[a, k // 2, pl.ds((k % 2) * rows, rows)]

    sends = []

    def q_go(a, src, step):
        k = src ^ step
        c = remote(
            q_slot(a, src), q_slot(a, k), qg_ssem.at[a, k], qg_rsem.at[a, k], q_mask(step)
        )
        c.start()
        sends.append(c)

    def k_go(a, src, step):
        j = src ^ step
        c = remote(
            kv.at[a, src], kv.at[a, j], kv_ssem.at[a, j], kv_rsem.at[a, j], k_mask(step)
        )
        c.start()
        sends.append(c)

    def q_wait(a, k):
        pltpu.make_async_copy(q_slot(a, k), q_slot(a, k), qg_rsem.at[a, k]).wait()

    def k_wait(a, j):
        pltpu.make_async_copy(kv.at[a, j], kv.at[a, j], kv_rsem.at[a, j]).wait()

    def tile(p, j):
        s = dot_nt(kv[0, j], qg[0, p]) * scale2
        m = jnp.max(s, axis=0, keepdims=True)
        e = jnp.exp2(s - m)
        gw = dot_nt(kv[1, j], qg[1, p])
        e_s[j, p] = e
        gw_s[j, p] = gw
        mlr[j, p, 0:1] = m
        mlr[j, p, 1:2] = jnp.sum(e, axis=0, keepdims=True)
        mlr[j, p, 2:3] = jnp.sum(e * gw, axis=0, keepdims=True)

    def tiles(ps, js):
        n = len(js)

        def step(i, carry):
            tile(ps[0] + i // n, js[0] + i % n)
            return carry

        lax.fori_loop(0, len(ps) * n, step, 0)

    def statistics(p):
        ms = [mlr[j, p, 0:1] for j in range(NK)]
        top = functools.reduce(jnp.maximum, ms)
        fs = [jnp.exp2(m - top) for m in ms]
        tot = sum(mlr[j, p, 1:2] * fs[j] for j in range(NK))
        dot = sum(mlr[j, p, 2:3] * fs[j] for j in range(NK))
        for n, val in enumerate((top + log2(tot), dot / tot)):
            st_send[0, p, n : n + 1] = val
            st_send[1, p, n : n + 1] = jnp.concatenate([val[:, rows:], val[:, :rows]], axis=1)

    def statistics_go(first, count, n):
        for k in range(1, NQ):
            part = pl.ds(first, count)
            remote(
                st_send.at[k % 2, part], st_all.at[k, part], st_ssem.at[n], st_rsem.at[n],
                q_mask(k),
            ).start()

    for a in (0, 1):
        k_go(a, 0, 2)
        q_go(a, 0, 2)
    for a in (0, 1):
        q_go(a, 0, 4)
        k_go(a, 0, 1)
    for a in (0, 1):
        q_go(a, 0, 1)
    for a in (0, 1):
        q_wait(a, 2)
        q_go(a, 2, 4)
        q_go(a, 2, 1)
        k_wait(a, 2)
        k_go(a, 2, 1)
    for a in (0, 1):
        q_wait(a, 1)
    tiles((0,), (0,))
    for a in (0, 1):
        q_wait(a, 4)
        q_go(a, 4, 1)
    for a in (0, 1):
        k_wait(a, 1)
    tiles((0,), (1, 2))
    for a in (0, 1):
        q_wait(a, 6)
        q_go(a, 6, 1)
    for a in (0, 1):
        q_wait(a, 3)
        q_wait(a, 5)
    tiles((1, 2), (0, 1, 2))
    for a in (0, 1):
        k_wait(a, 3)
    tiles((0, 1, 2), (3,))
    for p in range(NP - 1):
        statistics(p)
    statistics_go(0, NP - 1, 0)
    for a in (0, 1):
        q_wait(a, 7)
    tiles((3,), (0, 1, 2, 3))
    statistics(NP - 1)
    statistics_go(NP - 1, 1, 1)

    st_all[0] = st_send[0]
    keys_t = jnp.concatenate([kv[0, j].astype(F32).T for j in range(NK)], axis=1).astype(BF16)
    early, late = st_all.at[pl.ds(0, NQ - 1), pl.ds(0, NP - 1)], st_all.at[pl.ds(0, NQ - 1), pl.ds(0, 1)]
    pltpu.make_async_copy(early, early, st_rsem.at[0]).wait()
    pltpu.make_async_copy(late, late, st_rsem.at[1]).wait()
    for p in range(NP):
        got = [st_all[k, p ^ (k >> 1)] for k in range(NQ)]
        tops = [x[0:1] for x in got]
        top = functools.reduce(jnp.maximum, tops)
        total = top + log2(sum(jnp.exp2(x - top) for x in tops))
        fin[p, 0:1] = total
        fin[p, 1:2] = sum(jnp.exp2(x[0:1] - total) * x[1:2] for x in got)

    for j in (3, 2, 1, 0):
        dk = jnp.zeros((rows, D), F32)
        dv = jnp.zeros((rows, D), F32)
        for p in range(NP):
            w = e_s[j, p] * jnp.exp2(mlr[j, p, 0:1] - fin[p, 0:1])
            gl = (w * (gw_s[j, p] - fin[p, 1:2])).astype(BF16)
            gl_s[j, p] = gl
            dv = dv + jnp.dot(w.astype(BF16), qg[1, p], preferred_element_type=F32)
            dk = dk + jnp.dot(gl, qg[0, p], preferred_element_type=F32)
        buf = dkv_send if j else dkv_recv
        buf[j, 0] = (dk * scale).astype(BF16)
        buf[j, 1] = dv.astype(BF16)
        if j:
            remote(dkv_send.at[j], dkv_recv.at[j], dkv_ssem, dkv_rsem, k_mask(j)).start()

    for p in (3, 2, 1, 0):
        gl = jnp.concatenate([gl_s[j, p] for j in range(NK)], axis=0)
        dq = (jnp.dot(keys_t, gl, preferred_element_type=F32) * scale).T.astype(BF16)
        for k in (2 * p + 1, 2 * p):
            part = dq[(k % 2) * rows : (k % 2 + 1) * rows]
            if k:
                dq_send[k] = part
                remote(dq_send.at[k], dq_recv.at[k], dq_ssem, dq_rsem, q_mask(k)).start()
            else:
                dq_recv[0] = part

    pltpu.make_async_copy(
        dkv_recv.at[pl.ds(0, NK - 1)], dkv_recv.at[pl.ds(0, NK - 1)], dkv_rsem
    ).wait()
    dk = sum(dkv_recv[j, 0].astype(F32) for j in range(NK)).astype(BF16)
    dv = sum(dkv_recv[j, 1].astype(F32) for j in range(NK)).astype(BF16)
    pltpu.make_async_copy(
        dq_recv.at[pl.ds(0, NQ - 1)], dq_recv.at[pl.ds(0, NQ - 1)], dq_rsem
    ).wait()
    dq = sum(dq_recv[k].astype(F32) for k in range(NQ)).astype(BF16)

    for m in range(nu // GROUP):
        lo, hi = m * piece, (m + 1) * piece
        x = jnp.concatenate([dq[lo:hi], dk[lo:hi], dv[lo:hi]], axis=0)
        s = jnp.dot(unsort_ref[...], x, preferred_element_type=F32).astype(BF16)
        osend[m * GROUP : (m + 1) * GROUP] = s.reshape(GROUP, pack, D)
    for i in range(nu - 1, 0, -1):
        remote(osend.at[i], orecv.at[head], out_send, out_recv, h_mask(i)).start()
    orecv[head] = osend[0]
    pltpu.make_async_copy(
        orecv.at[pl.ds(0, nu - 1)], orecv.at[pl.ds(0, nu - 1)], out_recv
    ).wait()
    for h in range(nu):
        x = orecv[h].astype(F32)
        dq_ref[:, h * D : (h + 1) * D] = x[0:t].astype(BF16)
        dk_ref[:, h * D : (h + 1) * D] = x[t : 2 * t].astype(BF16)
        dv_ref[:, h * D : (h + 1) * D] = x[2 * t : 3 * t].astype(BF16)

    for view, sem in (
        (sbuf.at[pl.ds(0, nu - 1)], a2a_send), (early, st_ssem.at[0]), (late, st_ssem.at[1]),
        (dkv_send.at[pl.ds(0, NK - 1)], dkv_ssem), (dq_send.at[pl.ds(0, NQ - 1)], dq_ssem),
        (osend.at[pl.ds(0, nu - 1)], out_send),
    ):
        pltpu.make_async_copy(view, view, sem).wait()
    for c in sends:
        c.wait_send()


def sort_matrices(t):
    n = GROUP * t
    sort = np.zeros((4 * n, 4 * n), np.float32)
    for a in range(4):
        for g in range(GROUP):
            for i in range(t):
                sort[a * n + g * t + i, g * 4 * t + a * t + i] = 1.0
    return jnp.asarray(sort, BF16), jnp.asarray(sort[: 3 * n].T, BF16)


def local(nu, queries, key_vectors, value_vectors, cotangent):
    t = queries.shape[0]
    rows = nu * t
    cols = 2 * rows
    sort, unsort = sort_matrices(t)
    vmem = pl.BlockSpec(memory_space=pltpu.VMEM)
    hbm = pl.BlockSpec(memory_space=pltpu.HBM)
    out = jax.ShapeDtypeStruct(queries.shape, BF16)
    dma = pltpu.SemaphoreType.DMA
    args = [
        pltpu.with_memory_space_constraint(x, pltpu.HBM)
        for x in (queries, key_vectors, value_vectors, cotangent, sort, unsort)
    ]
    return pl.pallas_call(
        functools.partial(kernel, nu, t),
        out_shape=(out, out, out),
        in_specs=[hbm] * 6,
        out_specs=(vmem, vmem, vmem),
        scratch_shapes=[
            pltpu.VMEM((4, *queries.shape), BF16),
            pltpu.VMEM(sort.shape, BF16),
            pltpu.VMEM(unsort.shape, BF16),
            pltpu.VMEM((nu, 4 * t, D), BF16),
            pltpu.VMEM((nu, 4 * t, D), BF16),
            pltpu.VMEM((2, NP, cols, D), BF16),
            pltpu.VMEM((2, NK, rows, D), BF16),
            pltpu.VMEM((NK, NP, rows, cols), F32),
            pltpu.VMEM((NK, NP, rows, cols), F32),
            pltpu.VMEM((NK, NP, rows, cols), BF16),
            pltpu.VMEM((NK, NP, 8, cols), F32),
            pltpu.VMEM((NP, 8, cols), F32),
            pltpu.VMEM((2, NP, 2, cols), F32),
            pltpu.VMEM((NQ, NP, 2, cols), F32),
            pltpu.VMEM((NQ, rows, D), BF16),
            pltpu.VMEM((NQ, rows, D), BF16),
            pltpu.VMEM((NK, 2, rows, D), BF16),
            pltpu.VMEM((NK, 2, rows, D), BF16),
            pltpu.VMEM((nu, 4 * t, D), BF16),
            pltpu.VMEM((nu, 4 * t, D), BF16),
            dma((4,)), dma((2,)), dma, dma,
            dma((2, NK)), dma((2, NK)), dma((2, NQ)), dma((2, NQ)),
            dma((2,)), dma((2,)), dma, dma, dma, dma, dma, dma,
        ],
        compiler_params=pltpu.CompilerParams(
            collective_id=0, has_side_effects=True, vmem_limit_bytes=48 << 20
        ),
    )(*args)


def solution(mesh):
    placed = P(("blk", "ulysses"), None)
    return jax.shard_map(
        functools.partial(local, mesh.shape["ulysses"]),
        mesh=mesh,
        in_specs=(placed,) * 4,
        out_specs=(placed,) * 3,
        check_vma=False,
    )
```

```python
import functools
import math

import jax
import jax.numpy as jnp
import numpy as np
from jax import lax
from jax.experimental import pallas as pl
from jax.experimental.pallas import tpu as pltpu
from jax.sharding import PartitionSpec as P

D = 128
NQ = 8
NK = 4
NP = NQ // 2
F32 = jnp.float32
BF16 = jnp.bfloat16
GROUP = 8


def dot_nt(a, b):
    return lax.dot_general(a, b, (((1,), (1,)), ((), ())), preferred_element_type=F32)


def log2(x):
    return jnp.log(x) * (1.0 / math.log(2.0))


def q_mask(k):
    return (k >> 1) & 1, (k & 1) | ((k >> 2) & 1) << 1


def k_mask(j):
    return (j & 1) << 2 | (j >> 1) << 1, 0


def h_mask(i):
    iz, ix, iy = i >> 4, (i >> 2) & 3, i & 3
    mb = iy << 3 | (4 if iy == 2 else 0) | (2 if iz else 0)
    mu = iz << 4 | ix << 2 | (2 if ix == 2 else 0)
    return mb, mu


def kernel(
    nu, t, q_hbm, k_hbm, v_hbm, g_hbm, sort_hbm, unsort_hbm, dq_ref, dk_ref, dv_ref,
    stage, sort_ref, unsort_ref, sbuf, rbuf, qg, kv, e_s, gw_s, gl_s, mlr, fin, st_send, st_all,
    dq_send, dq_recv, dq_part, dq_own, dkv_send, dkv_recv, dkv_own, osend, orecv,
    stage_sem, sort_sem, a2a_send, a2a_recv, kv_ssem, kv_rsem, qg_ssem, qg_rsem,
    st_ssem, st_rsem, dq_ssem, dq_rsem, dkv_ssem, dkv_rsem, out_send, out_recv,
):
    rows = nu * t
    cols = 2 * rows
    pack = 4 * t
    u = lax.axis_index("ulysses")
    blk = lax.axis_index("blk")
    scale = 1.0 / math.sqrt(D)
    scale2 = scale * math.log2(math.e)

    def flips(value):
        return [(1 - 2 * ((value // (1 << b)) % 2)) * (1 << b) for b in range(5)]

    def flipped(value, flip, mask):
        for b in range(5):
            if mask >> b & 1:
                value = value + flip[b]
        return value

    blk_flip, u_flip = flips(blk), flips(u)
    head = (u // 16) * 16 + ((u // 4) % 4) * 4 + blk // 8
    head_flip = flips(head)

    def peer(masks):
        return {"blk": flipped(blk, blk_flip, masks[0]), "ulysses": flipped(u, u_flip, masks[1])}

    def remote(src, dst, ssem, rsem, masks):
        return pltpu.make_async_remote_copy(
            src_ref=src, dst_ref=dst, send_sem=ssem, recv_sem=rsem,
            device_id=peer(masks), device_id_type=pl.DeviceIdType.MESH,
        )

    loads = [
        pltpu.make_async_copy(src, stage.at[a], stage_sem.at[a])
        for a, src in enumerate((q_hbm, k_hbm, v_hbm, g_hbm))
    ]
    loads.append(pltpu.make_async_copy(sort_hbm, sort_ref, sort_sem.at[0]))
    loads.append(pltpu.make_async_copy(unsort_hbm, unsort_ref, sort_sem.at[1]))
    for c in loads:
        c.start()

    barrier = pltpu.get_barrier_semaphore()
    partners = [h_mask(i) for i in range(1, nu)]
    partners += [q_mask(k) for k in range(1, NQ)] + [k_mask(j) for j in range(1, NK)]
    for masks in partners:
        pl.semaphore_signal(
            barrier, inc=1, device_id=peer(masks), device_id_type=pl.DeviceIdType.MESH
        )

    for c in loads:
        c.wait()
    packed = jnp.concatenate([stage[a].astype(F32) for a in range(4)], axis=0).astype(BF16)
    for h in range(nu):
        sbuf[h] = packed[:, h * D : (h + 1) * D]
    rbuf[0] = sbuf[head]

    pl.semaphore_wait(barrier, len(partners))

    for i in range(nu - 1, 0, -1):
        remote(
            sbuf.at[flipped(head, head_flip, i)], rbuf.at[i], a2a_send, a2a_recv, h_mask(i)
        ).start()
    pltpu.make_async_copy(
        rbuf.at[pl.ds(0, nu - 1)], rbuf.at[pl.ds(0, nu - 1)], a2a_recv
    ).wait()

    piece = GROUP * t
    for m in range(nu // GROUP):
        x = rbuf[m * GROUP : (m + 1) * GROUP].reshape(GROUP * pack, D)
        s = jnp.dot(sort_ref[...], x, preferred_element_type=F32).astype(BF16)
        lo, hi = m * piece, (m + 1) * piece
        qg[0, 0, lo:hi, :] = s[0:piece]
        kv[0, 0, lo:hi, :] = s[piece : 2 * piece]
        kv[1, 0, lo:hi, :] = s[2 * piece : 3 * piece]
        qg[1, 0, lo:hi, :] = s[3 * piece : 4 * piece]

    def q_slot(a, k):
        return qg.at[a, k // 2, pl.ds((k % 2) * rows, rows)]

    sends = []

    def q_go(a, src, step):
        k = src ^ step
        c = remote(
            q_slot(a, src), q_slot(a, k), qg_ssem.at[a, k], qg_rsem.at[a, k], q_mask(step)
        )
        c.start()
        sends.append(c)

    def k_go(a, src, step):
        j = src ^ step
        c = remote(
            kv.at[a, src], kv.at[a, j], kv_ssem.at[a, j], kv_rsem.at[a, j], k_mask(step)
        )
        c.start()
        sends.append(c)

    def q_wait(a, k):
        pltpu.make_async_copy(q_slot(a, k), q_slot(a, k), qg_rsem.at[a, k]).wait()

    def k_wait(a, j):
        pltpu.make_async_copy(kv.at[a, j], kv.at[a, j], kv_rsem.at[a, j]).wait()

    def tile(p, j):
        s = dot_nt(kv[0, j], qg[0, p]) * scale2
        m = jnp.max(s, axis=0, keepdims=True)
        e = jnp.exp2(s - m)
        gw = dot_nt(kv[1, j], qg[1, p])
        e_s[j, p] = e
        gw_s[j, p] = gw
        mlr[j, p, 0:1] = m
        mlr[j, p, 1:2] = jnp.sum(e, axis=0, keepdims=True)
        mlr[j, p, 2:3] = jnp.sum(e * gw, axis=0, keepdims=True)

    def tiles(ps, js):
        n = len(js)

        def step(i, carry):
            tile(ps[0] + i // n, js[0] + i % n)
            return carry

        lax.fori_loop(0, len(ps) * n, step, 0)

    def statistics(p):
        ms = [mlr[j, p, 0:1] for j in range(NK)]
        top = functools.reduce(jnp.maximum, ms)
        fs = [jnp.exp2(m - top) for m in ms]
        tot = sum(mlr[j, p, 1:2] * fs[j] for j in range(NK))
        dot = sum(mlr[j, p, 2:3] * fs[j] for j in range(NK))
        for n, val in enumerate((top + log2(tot), dot / tot)):
            st_send[0, p, n : n + 1] = val
            st_send[1, p, n : n + 1] = jnp.concatenate([val[:, rows:], val[:, :rows]], axis=1)

    def statistics_go(first, count, n):
        for k in range(1, NQ):
            part = pl.ds(first, count)
            remote(
                st_send.at[k % 2, part], st_all.at[k, part], st_ssem.at[n], st_rsem.at[n],
                q_mask(k),
            ).start()

    for a in (0, 1):
        k_go(a, 0, 2)
        q_go(a, 0, 2)
    for a in (0, 1):
        q_go(a, 0, 4)
        k_go(a, 0, 1)
    for a in (0, 1):
        q_go(a, 0, 1)
    for a in (0, 1):
        q_wait(a, 2)
        q_go(a, 2, 4)
        q_go(a, 2, 1)
        k_wait(a, 2)
        k_go(a, 2, 1)
    for a in (0, 1):
        q_wait(a, 1)
    tiles((0,), (0,))
    for a in (0, 1):
        q_wait(a, 4)
        q_go(a, 4, 1)
    for a in (0, 1):
        k_wait(a, 1)
    tiles((0,), (1, 2))
    for a in (0, 1):
        q_wait(a, 6)
        q_go(a, 6, 1)
    for a in (0, 1):
        q_wait(a, 3)
        q_wait(a, 5)
    tiles((1, 2), (0, 1, 2))
    for a in (0, 1):
        k_wait(a, 3)
    tiles((0, 1, 2), (3,))
    for p in range(NP - 1):
        statistics(p)
    statistics_go(0, NP - 1, 0)
    for a in (0, 1):
        q_wait(a, 7)
    tiles((3,), (0, 1, 2, 3))
    statistics(NP - 1)
    statistics_go(NP - 1, 1, 1)

    st_all[0] = st_send[0]
    keys_t = jnp.concatenate([kv[0, j].astype(F32).T for j in range(NK)], axis=1).astype(BF16)
    early, late = st_all.at[pl.ds(0, NQ - 1), pl.ds(0, NP - 1)], st_all.at[pl.ds(0, NQ - 1), pl.ds(0, 1)]
    pltpu.make_async_copy(early, early, st_rsem.at[0]).wait()
    pltpu.make_async_copy(late, late, st_rsem.at[1]).wait()
    for p in range(NP):
        got = [st_all[k, p ^ (k >> 1)] for k in range(NQ)]
        tops = [x[0:1] for x in got]
        top = functools.reduce(jnp.maximum, tops)
        total = top + log2(sum(jnp.exp2(x - top) for x in tops))
        fin[p, 0:1] = total
        fin[p, 1:2] = sum(jnp.exp2(x[0:1] - total) * x[1:2] for x in got)

    for j in (3, 1, 2, 0):
        dk = jnp.zeros((rows, D), F32)
        dv = jnp.zeros((rows, D), F32)
        for p in range(NP):
            w = e_s[j, p] * jnp.exp2(mlr[j, p, 0:1] - fin[p, 0:1])
            gl = (w * (gw_s[j, p] - fin[p, 1:2])).astype(BF16)
            gl_s[j, p] = gl
            dv = dv + jnp.dot(w.astype(BF16), qg[1, p], preferred_element_type=F32)
            dk = dk + jnp.dot(gl, qg[0, p], preferred_element_type=F32)
        if j % 2:
            dkv_send[j, 0] = (dk * scale).astype(BF16)
            dkv_send[j, 1] = dv.astype(BF16)
            c = remote(
                dkv_send.at[j], dkv_recv.at[j ^ 1], dkv_ssem.at[j], dkv_rsem.at[j ^ 1], k_mask(1)
            )
            c.start()
            sends.append(c)
        else:
            dkv_own[j // 2, 0] = dk * scale
            dkv_own[j // 2, 1] = dv

    for p in (3, 2, 1, 0):
        gl = jnp.concatenate([gl_s[j, p] for j in range(NK)], axis=0)
        dq = (jnp.dot(keys_t, gl, preferred_element_type=F32) * scale).T
        if p >= 2:
            dq_send[p] = dq.astype(BF16)
            c = remote(
                dq_send.at[p], dq_recv.at[p - 2], dq_ssem.at[p], dq_rsem.at[p - 2], q_mask(4)
            )
            c.start()
            sends.append(c)
        else:
            dq_own[p] = dq

    def landed(ref, sem):
        pltpu.make_async_copy(ref, ref, sem).wait()

    landed(dkv_recv.at[2], dkv_rsem.at[2])
    dkv_send[2] = (dkv_own[1] + dkv_recv[2].astype(F32)).astype(BF16)
    c = remote(dkv_send.at[2], dkv_recv.at[1], dkv_ssem.at[2], dkv_rsem.at[1], k_mask(2))
    c.start()
    sends.append(c)
    for p in (1, 0):
        landed(dq_recv.at[p], dq_rsem.at[p])
        dq = dq_own[p] + dq_recv[p].astype(F32)
        dq_send[p] = dq.astype(BF16)
        for k in (2 * p, 2 * p + 1):
            if k:
                part = pl.ds((k % 2) * rows, rows)
                c = remote(
                    dq_send.at[p, part], dq_part.at[k], dq_ssem.at[3 + k], dq_rsem.at[1 + k],
                    q_mask(k),
                )
                c.start()
                sends.append(c)
    dq = dq[:rows]
    landed(dkv_recv.at[0], dkv_rsem.at[0])
    dkv = dkv_own[0] + dkv_recv[0].astype(F32)
    for k in (1, 2, 3):
        landed(dq_part.at[k], dq_rsem.at[1 + k])
        dq = dq + dq_part[k].astype(F32)
    dq = dq.astype(BF16)
    landed(dkv_recv.at[1], dkv_rsem.at[1])
    dkv = (dkv + dkv_recv[1].astype(F32)).astype(BF16)
    dk, dv = dkv[0], dkv[1]

    for m in range(nu // GROUP):
        lo, hi = m * piece, (m + 1) * piece
        x = jnp.concatenate([dq[lo:hi], dk[lo:hi], dv[lo:hi]], axis=0)
        s = jnp.dot(unsort_ref[...], x, preferred_element_type=F32).astype(BF16)
        osend[m * GROUP : (m + 1) * GROUP] = s.reshape(GROUP, pack, D)[:, : 3 * t]
    for i in range(nu - 1, 0, -1):
        remote(osend.at[i], orecv.at[head], out_send, out_recv, h_mask(i)).start()
    orecv[head] = osend[0]
    pltpu.make_async_copy(
        orecv.at[pl.ds(0, nu - 1)], orecv.at[pl.ds(0, nu - 1)], out_recv
    ).wait()
    for h in range(nu):
        x = orecv[h].astype(F32)
        dq_ref[:, h * D : (h + 1) * D] = x[0:t].astype(BF16)
        dk_ref[:, h * D : (h + 1) * D] = x[t : 2 * t].astype(BF16)
        dv_ref[:, h * D : (h + 1) * D] = x[2 * t : 3 * t].astype(BF16)

    for view, sem in (
        (sbuf.at[pl.ds(0, nu - 1)], a2a_send), (early, st_ssem.at[0]), (late, st_ssem.at[1]),
        (osend.at[pl.ds(0, nu - 1)], out_send),
    ):
        pltpu.make_async_copy(view, view, sem).wait()
    for c in sends:
        c.wait_send()


def sort_matrices(t):
    n = GROUP * t
    sort = np.zeros((4 * n, 4 * n), np.float32)
    for a in range(4):
        for g in range(GROUP):
            for i in range(t):
                sort[a * n + g * t + i, g * 4 * t + a * t + i] = 1.0
    return jnp.asarray(sort, BF16), jnp.asarray(sort[: 3 * n].T, BF16)


def local(nu, queries, key_vectors, value_vectors, cotangent):
    t = queries.shape[0]
    rows = nu * t
    cols = 2 * rows
    sort, unsort = sort_matrices(t)
    vmem = pl.BlockSpec(memory_space=pltpu.VMEM)
    hbm = pl.BlockSpec(memory_space=pltpu.HBM)
    out = jax.ShapeDtypeStruct(queries.shape, BF16)
    dma = pltpu.SemaphoreType.DMA
    args = [
        pltpu.with_memory_space_constraint(x, pltpu.HBM)
        for x in (queries, key_vectors, value_vectors, cotangent, sort, unsort)
    ]
    return pl.pallas_call(
        functools.partial(kernel, nu, t),
        out_shape=(out, out, out),
        in_specs=[hbm] * 6,
        out_specs=(vmem, vmem, vmem),
        scratch_shapes=[
            pltpu.VMEM((4, *queries.shape), BF16),
            pltpu.VMEM(sort.shape, BF16),
            pltpu.VMEM(unsort.shape, BF16),
            pltpu.VMEM((nu, 4 * t, D), BF16),
            pltpu.VMEM((nu, 4 * t, D), BF16),
            pltpu.VMEM((2, NP, cols, D), BF16),
            pltpu.VMEM((2, NK, rows, D), BF16),
            pltpu.VMEM((NK, NP, rows, cols), F32),
            pltpu.VMEM((NK, NP, rows, cols), F32),
            pltpu.VMEM((NK, NP, rows, cols), BF16),
            pltpu.VMEM((NK, NP, 8, cols), F32),
            pltpu.VMEM((NP, 8, cols), F32),
            pltpu.VMEM((2, NP, 2, cols), F32),
            pltpu.VMEM((NQ, NP, 2, cols), F32),
            pltpu.VMEM((NP, cols, D), BF16),
            pltpu.VMEM((2, cols, D), BF16),
            pltpu.VMEM((4, rows, D), BF16),
            pltpu.VMEM((2, cols, D), F32),
            pltpu.VMEM((NK, 2, rows, D), BF16),
            pltpu.VMEM((3, 2, rows, D), BF16),
            pltpu.VMEM((2, 2, rows, D), F32),
            pltpu.VMEM((nu, 3 * t, D), BF16),
            pltpu.VMEM((nu, 3 * t, D), BF16),
            dma((4,)), dma((2,)), dma, dma,
            dma((2, NK)), dma((2, NK)), dma((2, NQ)), dma((2, NQ)),
            dma((2,)), dma((2,)), dma((8,)), dma((8,)), dma((4,)), dma((4,)), dma, dma,
        ],
        compiler_params=pltpu.CompilerParams(
            collective_id=0, has_side_effects=True, vmem_limit_bytes=48 << 20
        ),
    )(*args)


def solution(mesh):
    placed = P(("blk", "ulysses"), None)
    return jax.shard_map(
        functools.partial(local, mesh.shape["ulysses"]),
        mesh=mesh,
        in_specs=(placed,) * 4,
        out_specs=(placed,) * 3,
        check_vma=False,
    )
```

```python
import functools
import math

import jax
import jax.numpy as jnp
import numpy as np
from jax import lax
from jax.experimental import pallas as pl
from jax.experimental.pallas import tpu as pltpu
from jax.sharding import PartitionSpec as P

D = 128
NQ = 8
NK = 4
NP = NQ // 2
F32 = jnp.float32
BF16 = jnp.bfloat16
GROUP = 8


def dot_nt(a, b):
    return lax.dot_general(a, b, (((1,), (1,)), ((), ())), preferred_element_type=F32)


def log2(x):
    return jnp.log(x) * (1.0 / math.log(2.0))


def q_mask(k):
    return (k >> 1) & 1, (k & 1) | ((k >> 2) & 1) << 1


def k_mask(j):
    return (j & 1) << 2 | (j >> 1) << 1, 0


def h_mask(i):
    iz, ix, iy = i >> 4, (i >> 2) & 3, i & 3
    mb = iy << 3 | (4 if iy == 2 else 0) | (2 if iz else 0)
    mu = iz << 4 | ix << 2 | (2 if ix == 2 else 0)
    return mb, mu


def kernel(
    nu, t, q_hbm, k_hbm, v_hbm, g_hbm, sort_hbm, unsort_hbm, dq_ref, dk_ref, dv_ref,
    stage, sort_ref, unsort_ref, sbuf, rbuf, qg, kv, e_s, gw_s, gl_s, mlr, fin, st_send, st_all,
    dq_send, dq_recv, dq_part, dq_own, dkv_send, dkv_recv, dkv_own, dkv_acc, osend, orecv,
    stage_sem, sort_sem, a2a_send, a2a_recv, kv_ssem, kv_rsem, qg_ssem, qg_rsem,
    st_ssem, st_rsem, dq_ssem, dq_rsem, dkv_ssem, dkv_rsem, out_send, out_recv,
):
    rows = nu * t
    cols = 2 * rows
    pack = 4 * t
    u = lax.axis_index("ulysses")
    blk = lax.axis_index("blk")
    scale = 1.0 / math.sqrt(D)
    scale2 = scale * math.log2(math.e)

    def flips(value):
        return [(1 - 2 * ((value // (1 << b)) % 2)) * (1 << b) for b in range(5)]

    def flipped(value, flip, mask):
        for b in range(5):
            if mask >> b & 1:
                value = value + flip[b]
        return value

    blk_flip, u_flip = flips(blk), flips(u)
    head = (u // 16) * 16 + ((u // 4) % 4) * 4 + blk // 8
    head_flip = flips(head)

    def peer(masks):
        return {"blk": flipped(blk, blk_flip, masks[0]), "ulysses": flipped(u, u_flip, masks[1])}

    def remote(src, dst, ssem, rsem, masks):
        return pltpu.make_async_remote_copy(
            src_ref=src, dst_ref=dst, send_sem=ssem, recv_sem=rsem,
            device_id=peer(masks), device_id_type=pl.DeviceIdType.MESH,
        )

    barrier = pltpu.get_barrier_semaphore()
    partners = [h_mask(i) for i in range(nu - 1, 0, -1)]
    partners += [q_mask(k) for k in range(1, NQ)] + [k_mask(j) for j in range(1, NK)]
    for masks in partners:
        pl.semaphore_signal(
            barrier, inc=1, device_id=peer(masks), device_id_type=pl.DeviceIdType.MESH
        )

    loads = [
        pltpu.make_async_copy(src, stage.at[a], stage_sem.at[a])
        for a, src in enumerate((q_hbm, k_hbm, v_hbm, g_hbm))
    ]
    loads.append(pltpu.make_async_copy(sort_hbm, sort_ref, sort_sem.at[0]))
    loads.append(pltpu.make_async_copy(unsort_hbm, unsort_ref, sort_sem.at[1]))
    for c in loads:
        c.start()

    for c in loads:
        c.wait()
    packed = jnp.concatenate([stage[a].astype(F32) for a in range(4)], axis=0).astype(BF16)
    for h in range(nu):
        sbuf[h] = packed[:, h * D : (h + 1) * D]
    rbuf[0] = sbuf[head]

    pl.semaphore_wait(barrier, len(partners))

    for i in range(nu - 1, 0, -1):
        remote(
            sbuf.at[flipped(head, head_flip, i)], rbuf.at[i], a2a_send,
            a2a_recv.at[i // GROUP], h_mask(i),
        ).start()

    def group_wait(buf, sem, m):
        first = max(m * GROUP, 1)
        part = buf.at[pl.ds(first, (m + 1) * GROUP - first)]
        pltpu.make_async_copy(part, part, sem.at[m]).wait()

    piece = GROUP * t
    for m in range(nu // GROUP):
        group_wait(rbuf, a2a_recv, m)
        x = rbuf[m * GROUP : (m + 1) * GROUP].reshape(GROUP * pack, D)
        s = jnp.dot(sort_ref[...], x, preferred_element_type=F32).astype(BF16)
        lo, hi = m * piece, (m + 1) * piece
        qg[0, 0, lo:hi, :] = s[0:piece]
        kv[0, 0, lo:hi, :] = s[piece : 2 * piece]
        kv[1, 0, lo:hi, :] = s[2 * piece : 3 * piece]
        qg[1, 0, lo:hi, :] = s[3 * piece : 4 * piece]

    def q_slot(a, k):
        return qg.at[a, k // 2, pl.ds((k % 2) * rows, rows)]

    sends = []

    def q_go(a, src, step):
        k = src ^ step
        c = remote(
            q_slot(a, src), q_slot(a, k), qg_ssem.at[a, k], qg_rsem.at[a, k], q_mask(step)
        )
        c.start()
        sends.append(c)

    def k_go(a, src, step):
        j = src ^ step
        c = remote(
            kv.at[a, src], kv.at[a, j], kv_ssem.at[a, j], kv_rsem.at[a, j], k_mask(step)
        )
        c.start()
        sends.append(c)

    def q_wait(a, k):
        pltpu.make_async_copy(q_slot(a, k), q_slot(a, k), qg_rsem.at[a, k]).wait()

    def k_wait(a, j):
        pltpu.make_async_copy(kv.at[a, j], kv.at[a, j], kv_rsem.at[a, j]).wait()

    def tile(p, j):
        s = dot_nt(kv[0, j], qg[0, p]) * scale2
        m = jnp.max(s, axis=0, keepdims=True)
        e = jnp.exp2(s - m)
        gw = dot_nt(kv[1, j], qg[1, p])
        e_s[j, p] = e
        gw_s[j, p] = gw
        mlr[j, p, 0:1] = m
        mlr[j, p, 1:2] = jnp.sum(e, axis=0, keepdims=True)
        mlr[j, p, 2:3] = jnp.sum(e * gw, axis=0, keepdims=True)

    def tiles(ps, js):
        n = len(js)

        def step(i, carry):
            tile(ps[0] + i // n, js[0] + i % n)
            return carry

        lax.fori_loop(0, len(ps) * n, step, 0)

    def statistics(p):
        ms = [mlr[j, p, 0:1] for j in range(NK)]
        top = functools.reduce(jnp.maximum, ms)
        fs = [jnp.exp2(m - top) for m in ms]
        tot = sum(mlr[j, p, 1:2] * fs[j] for j in range(NK))
        dot = sum(mlr[j, p, 2:3] * fs[j] for j in range(NK))
        for n, val in enumerate((top + log2(tot), dot / tot)):
            st_send[0, p, n : n + 1] = val
            st_send[1, p, n : n + 1] = jnp.concatenate([val[:, rows:], val[:, :rows]], axis=1)

    def statistics_go(first, count, n):
        for k in range(NQ - 1, 0, -1):
            part = pl.ds(first, count)
            remote(
                st_send.at[k % 2, part], st_all.at[k, part], st_ssem.at[n], st_rsem.at[n],
                q_mask(k),
            ).start()

    for a in (0, 1):
        q_go(a, 0, 2)
        k_go(a, 0, 2)
    for a in (0, 1):
        q_go(a, 0, 4)
        k_go(a, 0, 1)
    for a in (0, 1):
        q_go(a, 0, 1)
    for a in (0, 1):
        q_wait(a, 2)
        q_go(a, 2, 4)
        q_go(a, 2, 1)
        k_wait(a, 2)
        k_go(a, 2, 1)
    for a in (0, 1):
        q_wait(a, 1)
    tiles((0,), (0,))
    for a in (0, 1):
        q_wait(a, 4)
        q_go(a, 4, 1)
    for a in (0, 1):
        k_wait(a, 1)
    tiles((0,), (1, 2))
    for a in (0, 1):
        q_wait(a, 6)
        q_go(a, 6, 1)
    for a in (0, 1):
        q_wait(a, 3)
        q_wait(a, 5)
    tiles((1, 2), (0, 1, 2))
    for a in (0, 1):
        k_wait(a, 3)
    tiles((0, 1, 2), (3,))
    for p in range(NP - 1):
        statistics(p)
    statistics_go(0, NP - 1, 0)
    for a in (0, 1):
        q_wait(a, 7)
    tiles((3,), (0, 1, 2, 3))
    statistics(NP - 1)
    statistics_go(NP - 1, 1, 1)

    st_all[0] = st_send[0]
    keys_t = jnp.concatenate([kv[0, j].astype(F32).T for j in range(NK)], axis=1).astype(BF16)
    early, late = st_all.at[pl.ds(0, NQ - 1), pl.ds(0, NP - 1)], st_all.at[pl.ds(0, NQ - 1), pl.ds(0, 1)]
    pltpu.make_async_copy(early, early, st_rsem.at[0]).wait()
    pltpu.make_async_copy(late, late, st_rsem.at[1]).wait()
    for p in range(NP):
        got = [st_all[k, p ^ (k >> 1)] for k in range(NQ)]
        tops = [x[0:1] for x in got]
        top = functools.reduce(jnp.maximum, tops)
        total = top + log2(sum(jnp.exp2(x - top) for x in tops))
        fin[p, 0:1] = total
        fin[p, 1:2] = sum(jnp.exp2(x[0:1] - total) * x[1:2] for x in got)

    def adjoint(j, ps, dk, dv):
        for p in ps:
            w = e_s[j, p] * jnp.exp2(mlr[j, p, 0:1] - fin[p, 0:1])
            gl = (w * (gw_s[j, p] - fin[p, 1:2])).astype(BF16)
            gl_s[j, p] = gl
            dv = dv + jnp.dot(w.astype(BF16), qg[1, p], preferred_element_type=F32)
            dk = dk + jnp.dot(gl, qg[0, p], preferred_element_type=F32)
        return dk, dv

    def query_adjoint(p):
        gl = jnp.concatenate([gl_s[j, p] for j in range(NK)], axis=0)
        return (jnp.dot(keys_t, gl, preferred_element_type=F32) * scale).T

    for j in range(NK):
        zero = jnp.zeros((rows, D), F32)
        dkv_acc[j, 0], dkv_acc[j, 1] = adjoint(j, (3, 2), zero, zero)
    for p in (3, 2):
        dq_send[p] = query_adjoint(p).astype(BF16)
        c = remote(dq_send.at[p], dq_recv.at[p - 2], dq_ssem.at[p], dq_rsem.at[p - 2], q_mask(4))
        c.start()
        sends.append(c)
    for j in (3, 1, 2, 0):
        dk, dv = adjoint(j, (1, 0), dkv_acc[j, 0], dkv_acc[j, 1])
        if j % 2:
            dkv_send[j, 0] = (dk * scale).astype(BF16)
            dkv_send[j, 1] = dv.astype(BF16)
            c = remote(
                dkv_send.at[j], dkv_recv.at[j ^ 1], dkv_ssem.at[j], dkv_rsem.at[j ^ 1], k_mask(1)
            )
            c.start()
            sends.append(c)
        else:
            dkv_own[j // 2, 0] = dk * scale
            dkv_own[j // 2, 1] = dv
    for p in (1, 0):
        dq_own[p] = query_adjoint(p)

    def landed(ref, sem):
        pltpu.make_async_copy(ref, ref, sem).wait()

    landed(dkv_recv.at[2], dkv_rsem.at[2])
    dkv_send[2] = (dkv_own[1] + dkv_recv[2].astype(F32)).astype(BF16)
    c = remote(dkv_send.at[2], dkv_recv.at[1], dkv_ssem.at[2], dkv_rsem.at[1], k_mask(2))
    c.start()
    sends.append(c)
    for p in (1, 0):
        landed(dq_recv.at[p], dq_rsem.at[p])
        dq = dq_own[p] + dq_recv[p].astype(F32)
        dq_send[p] = dq.astype(BF16)
        for k in (2 * p, 2 * p + 1):
            if k:
                part = pl.ds((k % 2) * rows, rows)
                c = remote(
                    dq_send.at[p, part], dq_part.at[k], dq_ssem.at[3 + k], dq_rsem.at[1 + k],
                    q_mask(k),
                )
                c.start()
                sends.append(c)
    dq = dq[:rows]
    landed(dkv_recv.at[0], dkv_rsem.at[0])
    dkv = dkv_own[0] + dkv_recv[0].astype(F32)
    for k in (1, 2, 3):
        landed(dq_part.at[k], dq_rsem.at[1 + k])
        dq = dq + dq_part[k].astype(F32)
    dq = dq.astype(BF16)
    landed(dkv_recv.at[1], dkv_rsem.at[1])
    dkv = (dkv + dkv_recv[1].astype(F32)).astype(BF16)
    dk, dv = dkv[0], dkv[1]

    for m in range(nu // GROUP - 1, -1, -1):
        lo, hi = m * piece, (m + 1) * piece
        x = jnp.concatenate([dq[lo:hi], dk[lo:hi], dv[lo:hi]], axis=0)
        s = jnp.dot(unsort_ref[...], x, preferred_element_type=F32).astype(BF16)
        osend[m * GROUP : (m + 1) * GROUP] = s.reshape(GROUP, pack, D)[:, : 3 * t]
        for i in range((m + 1) * GROUP - 1, max(m * GROUP, 1) - 1, -1):
            remote(osend.at[i], orecv.at[i], out_send, out_recv.at[m], h_mask(i)).start()
    orecv[0] = osend[0]
    for m in range(nu // GROUP):
        group_wait(orecv, out_recv, m)
        for i in range(m * GROUP, (m + 1) * GROUP):
            at = pl.ds(pl.multiple_of(flipped(head, head_flip, i) * D, D), D)
            x = orecv[i].astype(F32)
            dq_ref[:, at] = x[0:t].astype(BF16)
            dk_ref[:, at] = x[t : 2 * t].astype(BF16)
            dv_ref[:, at] = x[2 * t : 3 * t].astype(BF16)

    for view, sem in (
        (sbuf.at[pl.ds(0, nu - 1)], a2a_send), (early, st_ssem.at[0]), (late, st_ssem.at[1]),
        (osend.at[pl.ds(0, nu - 1)], out_send),
    ):
        pltpu.make_async_copy(view, view, sem).wait()
    for c in sends:
        c.wait_send()


def sort_matrices(t):
    n = GROUP * t
    sort = np.zeros((4 * n, 4 * n), np.float32)
    for a in range(4):
        for g in range(GROUP):
            for i in range(t):
                sort[a * n + g * t + i, g * 4 * t + a * t + i] = 1.0
    return jnp.asarray(sort, BF16), jnp.asarray(sort[: 3 * n].T, BF16)


def local(nu, queries, key_vectors, value_vectors, cotangent):
    t = queries.shape[0]
    rows = nu * t
    cols = 2 * rows
    sort, unsort = sort_matrices(t)
    vmem = pl.BlockSpec(memory_space=pltpu.VMEM)
    hbm = pl.BlockSpec(memory_space=pltpu.HBM)
    out = jax.ShapeDtypeStruct(queries.shape, BF16)
    dma = pltpu.SemaphoreType.DMA
    args = [
        pltpu.with_memory_space_constraint(x, pltpu.HBM)
        for x in (queries, key_vectors, value_vectors, cotangent, sort, unsort)
    ]
    return pl.pallas_call(
        functools.partial(kernel, nu, t),
        out_shape=(out, out, out),
        in_specs=[hbm] * 6,
        out_specs=(vmem, vmem, vmem),
        scratch_shapes=[
            pltpu.VMEM((4, *queries.shape), BF16),
            pltpu.VMEM(sort.shape, BF16),
            pltpu.VMEM(unsort.shape, BF16),
            pltpu.VMEM((nu, 4 * t, D), BF16),
            pltpu.VMEM((nu, 4 * t, D), BF16),
            pltpu.VMEM((2, NP, cols, D), BF16),
            pltpu.VMEM((2, NK, rows, D), BF16),
            pltpu.VMEM((NK, NP, rows, cols), F32),
            pltpu.VMEM((NK, NP, rows, cols), F32),
            pltpu.VMEM((NK, NP, rows, cols), BF16),
            pltpu.VMEM((NK, NP, 8, cols), F32),
            pltpu.VMEM((NP, 8, cols), F32),
            pltpu.VMEM((2, NP, 2, cols), F32),
            pltpu.VMEM((NQ, NP, 2, cols), F32),
            pltpu.VMEM((NP, cols, D), BF16),
            pltpu.VMEM((2, cols, D), BF16),
            pltpu.VMEM((4, rows, D), BF16),
            pltpu.VMEM((2, cols, D), F32),
            pltpu.VMEM((NK, 2, rows, D), BF16),
            pltpu.VMEM((3, 2, rows, D), BF16),
            pltpu.VMEM((2, 2, rows, D), F32),
            pltpu.VMEM((NK, 2, rows, D), F32),
            pltpu.VMEM((nu, 3 * t, D), BF16),
            pltpu.VMEM((nu, 3 * t, D), BF16),
            dma((4,)), dma((2,)), dma, dma((nu // GROUP,)),
            dma((2, NK)), dma((2, NK)), dma((2, NQ)), dma((2, NQ)),
            dma((2,)), dma((2,)), dma((8,)), dma((8,)), dma((4,)), dma((4,)), dma, dma((nu // GROUP,)),
        ],
        compiler_params=pltpu.CompilerParams(
            collective_id=0, has_side_effects=True, vmem_limit_bytes=48 << 20
        ),
    )(*args)


def solution(mesh):
    placed = P(("blk", "ulysses"), None)
    return jax.shard_map(
        functools.partial(local, mesh.shape["ulysses"]),
        mesh=mesh,
        in_specs=(placed,) * 4,
        out_specs=(placed,) * 3,
        check_vma=False,
    )
```

```python
import functools
import math

import jax
import jax.numpy as jnp
import numpy as np
from jax import lax
from jax.experimental import pallas as pl
from jax.experimental.pallas import tpu as pltpu
from jax.sharding import PartitionSpec as P

D = 128
NQ = 8
NK = 4
NP = NQ // 2
F32 = jnp.float32
BF16 = jnp.bfloat16
GROUP = 8


def dot_nt(a, b):
    return lax.dot_general(a, b, (((1,), (1,)), ((), ())), preferred_element_type=F32)


def log2(x):
    return jnp.log(x) * (1.0 / math.log(2.0))


def q_mask(k):
    return (k >> 1) & 1, (k & 1) | ((k >> 2) & 1) << 1


def k_mask(j):
    return (j & 1) << 2 | (j >> 1) << 1, 0


def h_mask(i):
    iz, ix, iy = i >> 4, (i >> 2) & 3, i & 3
    mb = iy << 3 | (4 if iy == 2 else 0) | (2 if iz else 0)
    mu = iz << 4 | ix << 2 | (2 if ix == 2 else 0)
    return mb, mu


def kernel(
    nu, t, q_hbm, k_hbm, v_hbm, g_hbm, sort_hbm, unsort_hbm, out_ref,
    stage, sort_ref, unsort_ref, sbuf, rbuf, qg, kv, e_s, gw_s, gl_s, mlr, fin, st_send, st_all,
    dq_send, dq_recv, dq_part, dq_own, dkv_send, dkv_recv, dkv_own, dkv_acc, osend, orecv,
    stage_sem, sort_sem, a2a_send, a2a_recv, kv_ssem, kv_rsem, qg_ssem, qg_rsem,
    st_ssem, st_rsem, dq_ssem, dq_rsem, dkv_ssem, dkv_rsem, out_send, out_recv,
):
    rows = nu * t
    cols = 2 * rows
    pack = 4 * t
    u = lax.axis_index("ulysses")
    blk = lax.axis_index("blk")
    scale = 1.0 / math.sqrt(D)
    scale2 = scale * math.log2(math.e)

    def flips(value):
        return [(1 - 2 * ((value // (1 << b)) % 2)) * (1 << b) for b in range(5)]

    def flipped(value, flip, mask):
        for b in range(5):
            if mask >> b & 1:
                value = value + flip[b]
        return value

    blk_flip, u_flip = flips(blk), flips(u)
    head = (u // 16) * 16 + ((u // 4) % 4) * 4 + blk // 8
    head_flip = flips(head)

    def peer(masks):
        return {"blk": flipped(blk, blk_flip, masks[0]), "ulysses": flipped(u, u_flip, masks[1])}

    def remote(src, dst, ssem, rsem, masks):
        return pltpu.make_async_remote_copy(
            src_ref=src, dst_ref=dst, send_sem=ssem, recv_sem=rsem,
            device_id=peer(masks), device_id_type=pl.DeviceIdType.MESH,
        )

    barrier = pltpu.get_barrier_semaphore()
    partners = [h_mask(i) for i in range(nu - 1, 0, -1)]
    partners += [q_mask(k) for k in range(1, NQ)] + [k_mask(j) for j in range(1, NK)]
    for masks in partners:
        pl.semaphore_signal(
            barrier, inc=1, device_id=peer(masks), device_id_type=pl.DeviceIdType.MESH
        )

    loads = [
        pltpu.make_async_copy(src, stage.at[a], stage_sem.at[a])
        for a, src in enumerate((q_hbm, k_hbm, v_hbm, g_hbm))
    ]
    loads.append(pltpu.make_async_copy(sort_hbm, sort_ref, sort_sem.at[0]))
    loads.append(pltpu.make_async_copy(unsort_hbm, unsort_ref, sort_sem.at[1]))
    for c in loads:
        c.start()

    for c in loads:
        c.wait()
    packed = jnp.concatenate([stage[a].astype(F32) for a in range(4)], axis=0).astype(BF16)
    for h in range(nu):
        sbuf[h] = packed[:, h * D : (h + 1) * D]
    rbuf[0] = sbuf[head]

    pl.semaphore_wait(barrier, len(partners))

    for i in range(nu - 1, 0, -1):
        remote(
            sbuf.at[flipped(head, head_flip, i)], rbuf.at[i], a2a_send,
            a2a_recv.at[i // GROUP], h_mask(i),
        ).start()

    def group_wait(buf, sem, m):
        first = max(m * GROUP, 1)
        part = buf.at[pl.ds(first, (m + 1) * GROUP - first)]
        pltpu.make_async_copy(part, part, sem.at[m]).wait()

    piece = GROUP * t
    for m in range(nu // GROUP):
        group_wait(rbuf, a2a_recv, m)
        x = rbuf[m * GROUP : (m + 1) * GROUP].reshape(GROUP * pack, D)
        s = jnp.dot(sort_ref[...], x, preferred_element_type=F32).astype(BF16)
        lo, hi = m * piece, (m + 1) * piece
        qg[0, 0, lo:hi, :] = s[0:piece]
        kv[0, 0, lo:hi, :] = s[piece : 2 * piece]
        kv[1, 0, lo:hi, :] = s[2 * piece : 3 * piece]
        qg[1, 0, lo:hi, :] = s[3 * piece : 4 * piece]

    def q_slot(a, k):
        return qg.at[a, k // 2, pl.ds((k % 2) * rows, rows)]

    sends = []

    def q_go(a, src, step):
        k = src ^ step
        c = remote(
            q_slot(a, src), q_slot(a, k), qg_ssem.at[a, k], qg_rsem.at[a, k], q_mask(step)
        )
        c.start()
        sends.append(c)

    def k_slot(a, j, half):
        if half is None:
            return kv.at[a, j]
        return kv.at[a, j, pl.ds(half * (rows // 2), rows // 2)]

    def k_go(a, src, step, half=None):
        j, n = src ^ step, half or 0
        c = remote(
            k_slot(a, src, half), k_slot(a, j, half), kv_ssem.at[a, j, n], kv_rsem.at[a, j, n],
            k_mask(step),
        )
        c.start()
        sends.append(c)

    def q_wait(a, k):
        pltpu.make_async_copy(q_slot(a, k), q_slot(a, k), qg_rsem.at[a, k]).wait()

    def k_wait(a, j, half=None):
        part = k_slot(a, j, half)
        pltpu.make_async_copy(part, part, kv_rsem.at[a, j, half or 0]).wait()

    def tile(p, j):
        s = dot_nt(kv[0, j], qg[0, p]) * scale2
        m = jnp.max(s, axis=0, keepdims=True)
        e = jnp.exp2(s - m)
        gw = dot_nt(kv[1, j], qg[1, p])
        e_s[j, p] = e
        gw_s[j, p] = gw
        mlr[j, p, 0:1] = m
        mlr[j, p, 1:2] = jnp.sum(e, axis=0, keepdims=True)
        mlr[j, p, 2:3] = jnp.sum(e * gw, axis=0, keepdims=True)

    def tiles(ps, js):
        n = len(js)

        def step(i, carry):
            tile(ps[0] + i // n, js[0] + i % n)
            return carry

        lax.fori_loop(0, len(ps) * n, step, 0)

    def statistics(p):
        ms = [mlr[j, p, 0:1] for j in range(NK)]
        top = functools.reduce(jnp.maximum, ms)
        fs = [jnp.exp2(m - top) for m in ms]
        tot = sum(mlr[j, p, 1:2] * fs[j] for j in range(NK))
        dot = sum(mlr[j, p, 2:3] * fs[j] for j in range(NK))
        for n, val in enumerate((top + log2(tot), dot / tot)):
            st_send[0, p, n : n + 1] = val
            st_send[1, p, n : n + 1] = jnp.concatenate([val[:, rows:], val[:, :rows]], axis=1)

    def statistics_go(first, count, n):
        for k in range(NQ - 1, 0, -1):
            part = pl.ds(first, count)
            remote(
                st_send.at[k % 2, part], st_all.at[k, part], st_ssem.at[n], st_rsem.at[n],
                q_mask(k),
            ).start()

    for a in (0, 1):
        q_go(a, 0, 2)
        for half in (0, 1):
            k_go(a, 0, 2, half)
    for a in (0, 1):
        q_go(a, 0, 4)
        k_go(a, 0, 1)
    for a in (0, 1):
        q_go(a, 0, 1)
    for a in (0, 1):
        q_wait(a, 2)
        q_go(a, 2, 4)
        q_go(a, 2, 1)
        for half in (0, 1):
            k_wait(a, 2, half)
            k_go(a, 2, 1, half)
    for a in (0, 1):
        q_wait(a, 1)
    tiles((0,), (0,))
    for a in (0, 1):
        q_wait(a, 4)
        q_go(a, 4, 1)
    for a in (0, 1):
        k_wait(a, 1)
    tiles((0,), (1, 2))
    for a in (0, 1):
        q_wait(a, 6)
        q_go(a, 6, 1)
    for a in (0, 1):
        q_wait(a, 3)
        q_wait(a, 5)
    tiles((1, 2), (0, 1, 2))
    for a in (0, 1):
        for half in (0, 1):
            k_wait(a, 3, half)
    tiles((0, 1, 2), (3,))
    for p in range(NP - 1):
        statistics(p)
    statistics_go(0, NP - 1, 0)
    for a in (0, 1):
        q_wait(a, 7)
    tiles((3,), (0, 1, 2, 3))
    statistics(NP - 1)
    statistics_go(NP - 1, 1, 1)

    st_all[0] = st_send[0]
    keys_t = jnp.concatenate([kv[0, j].astype(F32).T for j in range(NK)], axis=1).astype(BF16)
    early, late = st_all.at[pl.ds(0, NQ - 1), pl.ds(0, NP - 1)], st_all.at[pl.ds(0, NQ - 1), pl.ds(0, 1)]
    pltpu.make_async_copy(early, early, st_rsem.at[0]).wait()
    pltpu.make_async_copy(late, late, st_rsem.at[1]).wait()
    for p in range(NP):
        got = [st_all[k, p ^ (k >> 1)] for k in range(NQ)]
        tops = [x[0:1] for x in got]
        top = functools.reduce(jnp.maximum, tops)
        total = top + log2(sum(jnp.exp2(x - top) for x in tops))
        fin[p, 0:1] = total
        fin[p, 1:2] = sum(jnp.exp2(x[0:1] - total) * x[1:2] for x in got)

    def adjoint(j, ps, dk, dv):
        for p in ps:
            w = e_s[j, p] * jnp.exp2(mlr[j, p, 0:1] - fin[p, 0:1])
            gl = (w * (gw_s[j, p] - fin[p, 1:2])).astype(BF16)
            gl_s[j, p] = gl
            dv = dv + jnp.dot(w.astype(BF16), qg[1, p], preferred_element_type=F32)
            dk = dk + jnp.dot(gl, qg[0, p], preferred_element_type=F32)
        return dk, dv

    def query_adjoint(p):
        gl = jnp.concatenate([gl_s[j, p] for j in range(NK)], axis=0)
        return (jnp.dot(keys_t, gl, preferred_element_type=F32) * scale).T

    for j in range(NK):
        zero = jnp.zeros((rows, D), F32)
        dkv_acc[j, 0], dkv_acc[j, 1] = adjoint(j, (3, 2), zero, zero)
    for p in (3, 2):
        dq_send[p] = query_adjoint(p).astype(BF16)
        c = remote(dq_send.at[p], dq_recv.at[p - 2], dq_ssem.at[p], dq_rsem.at[p - 2], q_mask(4))
        c.start()
        sends.append(c)
    for j in (3, 1, 2, 0):
        dk, dv = adjoint(j, (1, 0), dkv_acc[j, 0], dkv_acc[j, 1])
        if j % 2:
            dkv_send[j, 0] = (dk * scale).astype(BF16)
            dkv_send[j, 1] = dv.astype(BF16)
            c = remote(
                dkv_send.at[j], dkv_recv.at[j ^ 1], dkv_ssem.at[j], dkv_rsem.at[j ^ 1], k_mask(1)
            )
            c.start()
            sends.append(c)
        else:
            dkv_own[j // 2, 0] = dk * scale
            dkv_own[j // 2, 1] = dv
    for p in (1, 0):
        dq_own[p] = query_adjoint(p)

    def landed(ref, sem):
        pltpu.make_async_copy(ref, ref, sem).wait()

    landed(dkv_recv.at[2], dkv_rsem.at[2])
    dkv_send[2] = (dkv_own[1] + dkv_recv[2].astype(F32)).astype(BF16)
    c = remote(dkv_send.at[2], dkv_recv.at[1], dkv_ssem.at[2], dkv_rsem.at[1], k_mask(2))
    c.start()
    sends.append(c)
    for p in (1, 0):
        landed(dq_recv.at[p], dq_rsem.at[p])
        dq = dq_own[p] + dq_recv[p].astype(F32)
        dq_send[p] = dq.astype(BF16)
        for k in (2 * p, 2 * p + 1):
            if k:
                part = pl.ds((k % 2) * rows, rows)
                c = remote(
                    dq_send.at[p, part], dq_part.at[k], dq_ssem.at[3 + k], dq_rsem.at[1 + k],
                    q_mask(k),
                )
                c.start()
                sends.append(c)
    dq = dq[:rows]
    landed(dkv_recv.at[0], dkv_rsem.at[0])
    dkv = dkv_own[0] + dkv_recv[0].astype(F32)
    for k in (1, 2, 3):
        landed(dq_part.at[k], dq_rsem.at[1 + k])
        dq = dq + dq_part[k].astype(F32)
    dq = dq.astype(BF16)
    landed(dkv_recv.at[1], dkv_rsem.at[1])
    dkv = (dkv + dkv_recv[1].astype(F32)).astype(BF16)
    dk, dv = dkv[0], dkv[1]

    for m in range(nu // GROUP - 1, -1, -1):
        lo, hi = m * piece, (m + 1) * piece
        x = jnp.concatenate([dq[lo:hi], dk[lo:hi], dv[lo:hi]], axis=0)
        s = jnp.dot(unsort_ref[...], x, preferred_element_type=F32).astype(BF16)
        osend[m * GROUP : (m + 1) * GROUP] = s.reshape(GROUP, pack, D)[:, : 3 * t]
        for i in range((m + 1) * GROUP - 1, max(m * GROUP, 1) - 1, -1):
            remote(osend.at[i], orecv.at[i], out_send, out_recv.at[m], h_mask(i)).start()
    orecv[0] = osend[0]
    for m in range(nu // GROUP):
        group_wait(orecv, out_recv, m)
        for i in range(m * GROUP, (m + 1) * GROUP):
            at = pl.ds(pl.multiple_of(flipped(head, head_flip, i) * D, D), D)
            x = orecv[i].astype(F32)
            out_ref[0, :, at] = x[0:t].astype(BF16)
            out_ref[1, :, at] = x[t : 2 * t].astype(BF16)
            out_ref[2, :, at] = x[2 * t : 3 * t].astype(BF16)

    for view, sem in (
        (sbuf.at[pl.ds(0, nu - 1)], a2a_send), (early, st_ssem.at[0]), (late, st_ssem.at[1]),
        (osend.at[pl.ds(0, nu - 1)], out_send),
    ):
        pltpu.make_async_copy(view, view, sem).wait()
    for c in sends:
        c.wait_send()


def sort_matrices(t):
    n = GROUP * t
    sort = np.zeros((4 * n, 4 * n), np.float32)
    for a in range(4):
        for g in range(GROUP):
            for i in range(t):
                sort[a * n + g * t + i, g * 4 * t + a * t + i] = 1.0
    return jnp.asarray(sort, BF16), jnp.asarray(sort[: 3 * n].T, BF16)


def local(nu, queries, key_vectors, value_vectors, cotangent):
    t = queries.shape[0]
    rows = nu * t
    cols = 2 * rows
    sort, unsort = sort_matrices(t)
    vmem = pl.BlockSpec(memory_space=pltpu.VMEM)
    hbm = pl.BlockSpec(memory_space=pltpu.HBM)
    out = jax.ShapeDtypeStruct((3, *queries.shape), BF16)
    dma = pltpu.SemaphoreType.DMA
    args = [
        pltpu.with_memory_space_constraint(x, pltpu.HBM)
        for x in (queries, key_vectors, value_vectors, cotangent, sort, unsort)
    ]
    grads = pl.pallas_call(
        functools.partial(kernel, nu, t),
        out_shape=out,
        in_specs=[hbm] * 6,
        out_specs=vmem,
        scratch_shapes=[
            pltpu.VMEM((4, *queries.shape), BF16),
            pltpu.VMEM(sort.shape, BF16),
            pltpu.VMEM(unsort.shape, BF16),
            pltpu.VMEM((nu, 4 * t, D), BF16),
            pltpu.VMEM((nu, 4 * t, D), BF16),
            pltpu.VMEM((2, NP, cols, D), BF16),
            pltpu.VMEM((2, NK, rows, D), BF16),
            pltpu.VMEM((NK, NP, rows, cols), F32),
            pltpu.VMEM((NK, NP, rows, cols), F32),
            pltpu.VMEM((NK, NP, rows, cols), BF16),
            pltpu.VMEM((NK, NP, 8, cols), F32),
            pltpu.VMEM((NP, 8, cols), F32),
            pltpu.VMEM((2, NP, 2, cols), F32),
            pltpu.VMEM((NQ, NP, 2, cols), F32),
            pltpu.VMEM((NP, cols, D), BF16),
            pltpu.VMEM((2, cols, D), BF16),
            pltpu.VMEM((4, rows, D), BF16),
            pltpu.VMEM((2, cols, D), F32),
            pltpu.VMEM((NK, 2, rows, D), BF16),
            pltpu.VMEM((3, 2, rows, D), BF16),
            pltpu.VMEM((2, 2, rows, D), F32),
            pltpu.VMEM((NK, 2, rows, D), F32),
            pltpu.VMEM((nu, 3 * t, D), BF16),
            pltpu.VMEM((nu, 3 * t, D), BF16),
            dma((4,)), dma((2,)), dma, dma((nu // GROUP,)),
            dma((2, NK, 2)), dma((2, NK, 2)), dma((2, NQ)), dma((2, NQ)),
            dma((2,)), dma((2,)), dma((8,)), dma((8,)), dma((4,)), dma((4,)), dma, dma((nu // GROUP,)),
        ],
        compiler_params=pltpu.CompilerParams(
            collective_id=0, has_side_effects=True, vmem_limit_bytes=48 << 20
        ),
    )(*args)
    return grads[0], grads[1], grads[2]


def solution(mesh):
    placed = P(("blk", "ulysses"), None)
    return jax.shard_map(
        functools.partial(local, mesh.shape["ulysses"]),
        mesh=mesh,
        in_specs=(placed,) * 4,
        out_specs=(placed,) * 3,
        check_vma=False,
    )
```

```python
import functools
import math

import jax
import jax.numpy as jnp
import numpy as np
from jax import lax
from jax.experimental import pallas as pl
from jax.experimental.pallas import tpu as pltpu
from jax.sharding import PartitionSpec as P

D = 128
NQ = 8
NK = 4
NP = NQ // 2
F32 = jnp.float32
BF16 = jnp.bfloat16
GROUP = 8


def dot_nt(a, b):
    return lax.dot_general(a, b, (((1,), (1,)), ((), ())), preferred_element_type=F32)


def log2(x):
    return jnp.log(x) * (1.0 / math.log(2.0))


def q_mask(k):
    return (k >> 1) & 1, (k & 1) | ((k >> 2) & 1) << 1


def k_mask(j):
    return (j & 1) << 2 | (j >> 1) << 1, 0


def h_mask(i):
    iz, ix, iy = i >> 4, (i >> 2) & 3, i & 3
    mb = iy << 3 | (4 if iy == 2 else 0) | (2 if iz else 0)
    mu = iz << 4 | ix << 2 | (2 if ix == 2 else 0)
    return mb, mu


def kernel(
    nu, t, q_hbm, k_hbm, v_hbm, g_hbm, sort_hbm, unsort_hbm, out_ref,
    stage, sort_ref, unsort_ref, sbuf, rbuf, qg, kv, e_s, gw_s, gl_s, mlr, fin, st_send, st_all,
    dq_send, dq_recv, dq_part, dq_own, dkv_send, dkv_recv, dkv_own, dkv_acc, osend, orecv,
    stage_sem, sort_sem, a2a_send, a2a_recv, kv_ssem, kv_rsem, qg_ssem, qg_rsem,
    st_ssem, st_rsem, dq_ssem, dq_rsem, dkv_ssem, dkv_rsem, out_send, out_recv,
):
    rows = nu * t
    cols = 2 * rows
    pack = 4 * t
    u = lax.axis_index("ulysses")
    blk = lax.axis_index("blk")
    scale = 1.0 / math.sqrt(D)
    scale2 = scale * math.log2(math.e)

    def flips(value):
        return [(1 - 2 * ((value // (1 << b)) % 2)) * (1 << b) for b in range(5)]

    def flipped(value, flip, mask):
        for b in range(5):
            if mask >> b & 1:
                value = value + flip[b]
        return value

    blk_flip, u_flip = flips(blk), flips(u)
    head = (u // 16) * 16 + ((u // 4) % 4) * 4 + blk // 8
    head_flip = flips(head)

    def peer(masks):
        return {"blk": flipped(blk, blk_flip, masks[0]), "ulysses": flipped(u, u_flip, masks[1])}

    def remote(src, dst, ssem, rsem, masks):
        return pltpu.make_async_remote_copy(
            src_ref=src, dst_ref=dst, send_sem=ssem, recv_sem=rsem,
            device_id=peer(masks), device_id_type=pl.DeviceIdType.MESH,
        )

    barrier = pltpu.get_barrier_semaphore()
    partners = [h_mask(i) for i in range(nu - 1, 0, -1)]
    partners += [q_mask(k) for k in range(1, NQ)] + [k_mask(j) for j in range(1, NK)]
    for masks in partners:
        pl.semaphore_signal(
            barrier, inc=1, device_id=peer(masks), device_id_type=pl.DeviceIdType.MESH
        )

    loads = [
        pltpu.make_async_copy(src, stage.at[a], stage_sem.at[a])
        for a, src in enumerate((q_hbm, k_hbm, v_hbm, g_hbm))
    ]
    loads.append(pltpu.make_async_copy(sort_hbm, sort_ref, sort_sem.at[0]))
    loads.append(pltpu.make_async_copy(unsort_hbm, unsort_ref, sort_sem.at[1]))
    for c in loads:
        c.start()

    for c in loads:
        c.wait()
    packed = jnp.concatenate([stage[a].astype(F32) for a in range(4)], axis=0).astype(BF16)
    for h in range(nu):
        sbuf[h] = packed[:, h * D : (h + 1) * D]
    rbuf[0] = sbuf[head]

    pl.semaphore_wait(barrier, len(partners))

    for i in range(nu - 1, 0, -1):
        remote(
            sbuf.at[flipped(head, head_flip, i)], rbuf.at[i], a2a_send,
            a2a_recv.at[i // GROUP], h_mask(i),
        ).start()

    def group_wait(buf, sem, m):
        first = max(m * GROUP, 1)
        part = buf.at[pl.ds(first, (m + 1) * GROUP - first)]
        pltpu.make_async_copy(part, part, sem.at[m]).wait()

    piece = GROUP * t
    for m in range(nu // GROUP):
        group_wait(rbuf, a2a_recv, m)
        x = rbuf[m * GROUP : (m + 1) * GROUP].reshape(GROUP * pack, D)
        s = jnp.dot(sort_ref[...], x, preferred_element_type=F32).astype(BF16)
        lo, hi = m * piece, (m + 1) * piece
        qg[0, 0, lo:hi, :] = s[0:piece]
        kv[0, 0, lo:hi, :] = s[piece : 2 * piece]
        kv[1, 0, lo:hi, :] = s[2 * piece : 3 * piece]
        qg[1, 0, lo:hi, :] = s[3 * piece : 4 * piece]

    def q_slot(a, k):
        return qg.at[a, k // 2, pl.ds((k % 2) * rows, rows)]

    sends = []

    def q_go(a, src, step):
        k = src ^ step
        c = remote(
            q_slot(a, src), q_slot(a, k), qg_ssem.at[a, k], qg_rsem.at[a, k], q_mask(step)
        )
        c.start()
        sends.append(c)

    def k_slot(a, j, half):
        if half is None:
            return kv.at[a, j]
        return kv.at[a, j, pl.ds(half * (rows // 2), rows // 2)]

    def k_go(a, src, step, half=None):
        j, n = src ^ step, half or 0
        c = remote(
            k_slot(a, src, half), k_slot(a, j, half), kv_ssem.at[a, j, n], kv_rsem.at[a, j, n],
            k_mask(step),
        )
        c.start()
        sends.append(c)

    def q_wait(a, k):
        pltpu.make_async_copy(q_slot(a, k), q_slot(a, k), qg_rsem.at[a, k]).wait()

    def k_wait(a, j, half=None):
        part = k_slot(a, j, half)
        pltpu.make_async_copy(part, part, kv_rsem.at[a, j, half or 0]).wait()

    def tile(p, j):
        s = dot_nt(kv[0, j], qg[0, p]) * scale2
        m = jnp.max(s, axis=0, keepdims=True)
        e = jnp.exp2(s - m)
        gw = dot_nt(kv[1, j], qg[1, p])
        e_s[j, p] = e
        gw_s[j, p] = gw
        mlr[j, p, 0:1] = m
        mlr[j, p, 1:2] = jnp.sum(e, axis=0, keepdims=True)
        mlr[j, p, 2:3] = jnp.sum(e * gw, axis=0, keepdims=True)

    def tiles(ps, js):
        n = len(js)

        def step(i, carry):
            tile(ps[0] + i // n, js[0] + i % n)
            return carry

        lax.fori_loop(0, len(ps) * n, step, 0)

    def statistics(p):
        ms = [mlr[j, p, 0:1] for j in range(NK)]
        top = functools.reduce(jnp.maximum, ms)
        fs = [jnp.exp2(m - top) for m in ms]
        tot = sum(mlr[j, p, 1:2] * fs[j] for j in range(NK))
        dot = sum(mlr[j, p, 2:3] * fs[j] for j in range(NK))
        for n, val in enumerate((top + log2(tot), dot / tot)):
            st_send[0, p, n : n + 1] = val
            st_send[1, p, n : n + 1] = jnp.concatenate([val[:, rows:], val[:, :rows]], axis=1)

    def statistics_go(first, count, n):
        for k in range(NQ - 1, 0, -1):
            part = pl.ds(first, count)
            remote(
                st_send.at[k % 2, part], st_all.at[k, part], st_ssem.at[n], st_rsem.at[n],
                q_mask(k),
            ).start()

    for a in (0, 1):
        q_go(a, 0, 2)
        for half in (0, 1):
            k_go(a, 0, 2, half)
    for a in (0, 1):
        q_go(a, 0, 4)
        k_go(a, 0, 1)
    for a in (0, 1):
        q_go(a, 0, 1)
    for a in (0, 1):
        q_wait(a, 2)
        q_go(a, 2, 4)
        q_go(a, 2, 1)
        for half in (0, 1):
            k_wait(a, 2, half)
            k_go(a, 2, 1, half)
    for a in (0, 1):
        q_wait(a, 1)
    tiles((0,), (0,))
    for a in (0, 1):
        q_wait(a, 4)
        q_go(a, 4, 1)
    for a in (0, 1):
        k_wait(a, 1)
    tiles((0,), (1, 2))
    for a in (0, 1):
        q_wait(a, 6)
        q_go(a, 6, 1)
    for a in (0, 1):
        q_wait(a, 3)
        q_wait(a, 5)
    tiles((1, 2), (0, 1, 2))
    for a in (0, 1):
        for half in (0, 1):
            k_wait(a, 3, half)
    tiles((0, 1, 2), (3,))
    for p in range(NP - 1):
        statistics(p)
    statistics_go(0, NP - 1, 0)
    for a in (0, 1):
        q_wait(a, 7)
    tiles((3,), (0, 1, 2, 3))
    statistics(NP - 1)
    statistics_go(NP - 1, 1, 1)

    st_all[0] = st_send[0]
    keys_t = jnp.concatenate([kv[0, j].astype(F32).T for j in range(NK)], axis=1).astype(BF16)
    early, late = st_all.at[pl.ds(0, NQ - 1), pl.ds(0, NP - 1)], st_all.at[pl.ds(0, NQ - 1), pl.ds(0, 1)]
    pltpu.make_async_copy(early, early, st_rsem.at[0]).wait()
    pltpu.make_async_copy(late, late, st_rsem.at[1]).wait()
    for p in range(NP):
        got = [st_all[k, p ^ (k >> 1)] for k in range(NQ)]
        tops = [x[0:1] for x in got]
        top = functools.reduce(jnp.maximum, tops)
        total = top + log2(sum(jnp.exp2(x - top) for x in tops))
        fin[p, 0:1] = total
        fin[p, 1:2] = sum(jnp.exp2(x[0:1] - total) * x[1:2] for x in got)

    def adjoint(j, ps, dk, dv):
        for p in ps:
            w = e_s[j, p] * jnp.exp2(mlr[j, p, 0:1] - fin[p, 0:1])
            gl = (w * (gw_s[j, p] - fin[p, 1:2])).astype(BF16)
            gl_s[j, p] = gl
            dv = dv + jnp.dot(w.astype(BF16), qg[1, p], preferred_element_type=F32)
            dk = dk + jnp.dot(gl, qg[0, p], preferred_element_type=F32)
        return dk, dv

    def dkv_go(a, src, dst, step):
        c = remote(
            dkv_send.at[src, a], dkv_recv.at[dst, a], dkv_ssem.at[a, src], dkv_rsem.at[a, dst],
            k_mask(step),
        )
        c.start()
        sends.append(c)

    def query_adjoint(p):
        gl = jnp.concatenate([gl_s[j, p] for j in range(NK)], axis=0)
        return (jnp.dot(keys_t, gl, preferred_element_type=F32) * scale).T

    for j in range(NK):
        zero = jnp.zeros((rows, D), F32)
        dkv_acc[j, 0], dkv_acc[j, 1] = adjoint(j, (3, 2), zero, zero)
    for p in (3, 2):
        dq_send[p] = query_adjoint(p).astype(BF16)
        c = remote(dq_send.at[p], dq_recv.at[p - 2], dq_ssem.at[p], dq_rsem.at[p - 2], q_mask(4))
        c.start()
        sends.append(c)
    for j in (3, 1, 2, 0):
        dk, dv = adjoint(j, (1, 0), dkv_acc[j, 0], dkv_acc[j, 1])
        if j % 2:
            dkv_send[j, 0] = (dk * scale).astype(BF16)
            dkv_send[j, 1] = dv.astype(BF16)
            for a in (0, 1):
                dkv_go(a, j, j ^ 1, 1)
        else:
            dkv_own[j // 2, 0] = dk * scale
            dkv_own[j // 2, 1] = dv
    for p in (1, 0):
        dq_own[p] = query_adjoint(p)

    def landed(ref, sem):
        pltpu.make_async_copy(ref, ref, sem).wait()

    for a in (0, 1):
        landed(dkv_recv.at[2, a], dkv_rsem.at[a, 2])
        dkv_send[2, a] = (dkv_own[1, a] + dkv_recv[2, a].astype(F32)).astype(BF16)
        dkv_go(a, 2, 1, 2)
    for p in (1, 0):
        landed(dq_recv.at[p], dq_rsem.at[p])
        dq = dq_own[p] + dq_recv[p].astype(F32)
        dq_send[p] = dq.astype(BF16)
        for k in (2 * p, 2 * p + 1):
            if k:
                part = pl.ds((k % 2) * rows, rows)
                c = remote(
                    dq_send.at[p, part], dq_part.at[k], dq_ssem.at[3 + k], dq_rsem.at[1 + k],
                    q_mask(k),
                )
                c.start()
                sends.append(c)
    dq = dq[:rows]
    for a in (0, 1):
        landed(dkv_recv.at[0, a], dkv_rsem.at[a, 0])
    dkv = dkv_own[0] + dkv_recv[0].astype(F32)
    for k in (1, 2, 3):
        landed(dq_part.at[k], dq_rsem.at[1 + k])
        dq = dq + dq_part[k].astype(F32)
    dq = dq.astype(BF16)
    for a in (0, 1):
        landed(dkv_recv.at[1, a], dkv_rsem.at[a, 1])
    dkv = (dkv + dkv_recv[1].astype(F32)).astype(BF16)
    dk, dv = dkv[0], dkv[1]

    for m in range(nu // GROUP - 1, -1, -1):
        lo, hi = m * piece, (m + 1) * piece
        x = jnp.concatenate([dq[lo:hi], dk[lo:hi], dv[lo:hi]], axis=0)
        s = jnp.dot(unsort_ref[...], x, preferred_element_type=F32).astype(BF16)
        osend[m * GROUP : (m + 1) * GROUP] = s.reshape(GROUP, pack, D)[:, : 3 * t]
        for i in range((m + 1) * GROUP - 1, max(m * GROUP, 1) - 1, -1):
            remote(osend.at[i], orecv.at[i], out_send, out_recv.at[m], h_mask(i)).start()
    orecv[0] = osend[0]
    for m in range(nu // GROUP):
        group_wait(orecv, out_recv, m)
        for i in range(m * GROUP, (m + 1) * GROUP):
            at = pl.ds(pl.multiple_of(flipped(head, head_flip, i) * D, D), D)
            x = orecv[i].astype(F32)
            out_ref[0, :, at] = x[0:t].astype(BF16)
            out_ref[1, :, at] = x[t : 2 * t].astype(BF16)
            out_ref[2, :, at] = x[2 * t : 3 * t].astype(BF16)

    for view, sem in (
        (sbuf.at[pl.ds(0, nu - 1)], a2a_send), (early, st_ssem.at[0]), (late, st_ssem.at[1]),
        (osend.at[pl.ds(0, nu - 1)], out_send),
    ):
        pltpu.make_async_copy(view, view, sem).wait()
    for c in sends:
        c.wait_send()


def sort_matrices(t):
    n = GROUP * t
    sort = np.zeros((4 * n, 4 * n), np.float32)
    for a in range(4):
        for g in range(GROUP):
            for i in range(t):
                sort[a * n + g * t + i, g * 4 * t + a * t + i] = 1.0
    return jnp.asarray(sort, BF16), jnp.asarray(sort[: 3 * n].T, BF16)


def local(nu, queries, key_vectors, value_vectors, cotangent):
    t = queries.shape[0]
    rows = nu * t
    cols = 2 * rows
    sort, unsort = sort_matrices(t)
    vmem = pl.BlockSpec(memory_space=pltpu.VMEM)
    hbm = pl.BlockSpec(memory_space=pltpu.HBM)
    out = jax.ShapeDtypeStruct((3, *queries.shape), BF16)
    dma = pltpu.SemaphoreType.DMA
    args = [
        pltpu.with_memory_space_constraint(x, pltpu.HBM)
        for x in (queries, key_vectors, value_vectors, cotangent, sort, unsort)
    ]
    grads = pl.pallas_call(
        functools.partial(kernel, nu, t),
        out_shape=out,
        in_specs=[hbm] * 6,
        out_specs=vmem,
        scratch_shapes=[
            pltpu.VMEM((4, *queries.shape), BF16),
            pltpu.VMEM(sort.shape, BF16),
            pltpu.VMEM(unsort.shape, BF16),
            pltpu.VMEM((nu, 4 * t, D), BF16),
            pltpu.VMEM((nu, 4 * t, D), BF16),
            pltpu.VMEM((2, NP, cols, D), BF16),
            pltpu.VMEM((2, NK, rows, D), BF16),
            pltpu.VMEM((NK, NP, rows, cols), F32),
            pltpu.VMEM((NK, NP, rows, cols), F32),
            pltpu.VMEM((NK, NP, rows, cols), BF16),
            pltpu.VMEM((NK, NP, 8, cols), F32),
            pltpu.VMEM((NP, 8, cols), F32),
            pltpu.VMEM((2, NP, 2, cols), F32),
            pltpu.VMEM((NQ, NP, 2, cols), F32),
            pltpu.VMEM((NP, cols, D), BF16),
            pltpu.VMEM((2, cols, D), BF16),
            pltpu.VMEM((4, rows, D), BF16),
            pltpu.VMEM((2, cols, D), F32),
            pltpu.VMEM((NK, 2, rows, D), BF16),
            pltpu.VMEM((3, 2, rows, D), BF16),
            pltpu.VMEM((2, 2, rows, D), F32),
            pltpu.VMEM((NK, 2, rows, D), F32),
            pltpu.VMEM((nu, 3 * t, D), BF16),
            pltpu.VMEM((nu, 3 * t, D), BF16),
            dma((4,)), dma((2,)), dma, dma((nu // GROUP,)),
            dma((2, NK, 2)), dma((2, NK, 2)), dma((2, NQ)), dma((2, NQ)),
            dma((2,)), dma((2,)), dma((8,)), dma((8,)), dma((2, 4)), dma((2, 4)), dma, dma((nu // GROUP,)),
        ],
        compiler_params=pltpu.CompilerParams(
            collective_id=0, has_side_effects=True, vmem_limit_bytes=48 << 20
        ),
    )(*args)
    return grads[0], grads[1], grads[2]


def solution(mesh):
    placed = P(("blk", "ulysses"), None)
    return jax.shard_map(
        functools.partial(local, mesh.shape["ulysses"]),
        mesh=mesh,
        in_specs=(placed,) * 4,
        out_specs=(placed,) * 3,
        check_vma=False,
    )
```
